32 devices in a mesh: dom: 8 (over y, x, core), sec: 4 (over z).
Axes of the slice: x: 2, y: 2, z: 4, core: 2. Of those that a mesh axis runs over, the one named last changes fastest.
Arguments:
- wavefunction: bfloat16 [8, 8, 4, 128, 128], P('dom', 'sec'), may hold values from -6 to 6
- left_env: bfloat16 [8, 26, 8, 128, 128], P('dom', None, 'sec'), may hold values from -0.109375 to 0.109375
- right_env: bfloat16 [8, 26, 8, 128, 128], P('dom', None, 'sec'), may hold values from -0.5 to 0.5
- local_ops: bfloat16 [26, 4, 4], replicated, may hold values from -3 to 3
- targets: int32 [26, 8], replicated, may hold values from 0 to 7, as said below
Outputs:
- applied: bfloat16 [8, 8, 4, 128, 128], P('dom', 'sec')
The draws below stay inside these ranges and needn't reach their ends.
Inputs may be any that keep to these rules, and one draw needn't show every extreme that they name: Sector labels are periodic: targets[w,s] is s, (s + 1) mod 8, (s - 1) mod 8 or (s + 4) mod 8; the first MPO index keeps every sector (targets[0,s] = s) and the second moves every sector by 4.
All inputs are finite; a program needn't handle non-finite values.
Results may differ from the reference program's by a relative error of at most 0.01.
Values may be sent and summed in bfloat16 or wider, within the bound.
A program may use at most 128 MiB of HBM per device.

```python
import jax
import jax.numpy as jnp
from jax import lax

BLOCK = 128
PHYS = 4
TERMS = 26
REACH = 1
SEC_DEV = 2
SECTORS = 8
PARTITIONS = 8
N_SEC = 4


def draw_targets(key, part):
    sector_ids = jnp.arange(SECTORS, dtype=jnp.int32)[None, :]
    term_ids = jnp.arange(TERMS, dtype=jnp.int32)[:, None]
    options = jnp.array([-REACH, 0, REACH, SECTORS // 2], dtype=jnp.int32)
    picks = jax.random.randint(key, (TERMS, SECTORS), 0, 4, dtype=jnp.int32)
    charge_step = options[picks]
    charge_step = jnp.where(term_ids == 0, 0, charge_step)
    charge_step = jnp.where(term_ids == 1, SECTORS // 2, charge_step)
    charge_step = jnp.where(term_ids == 2, REACH, charge_step)
    charge_step = jnp.where(term_ids == 3, -REACH, charge_step)
    return ((sector_ids + charge_step + SECTORS) % SECTORS).astype(jnp.int32)


def steps_of(rng, extent, cuts, least, largest):
    def one(position, blocks):
        draws = jax.random.uniform(jax.random.fold_in(jax.random.fold_in(rng, 6), position), (blocks,), jnp.float32, least / len(cuts), largest / len(cuts))
        return jnp.repeat(jnp.exp(draws), extent[position] // blocks).reshape((-1,) + (1,) * (len(extent) - position - 1))

    gain = one(*cuts[0])
    for cut in cuts[1:]:
        gain = gain * one(*cut)
    return gain


def scatter_about(stream_key, dims, deviation, reach, split=(), kind=jnp.bfloat16):
    entries = deviation * jax.random.normal(stream_key, dims, jnp.float32)
    if split:
        entries = entries * steps_of(stream_key, dims, split, -0.22, 0.18)
    return jnp.clip(entries, -reach, reach).astype(kind)


def setup_inputs(seed: int = 0) -> dict:
    seeds = jax.random.split(jax.random.key(seed), 6)
    wavefunction = scatter_about(seeds[0], (PARTITIONS, SECTORS, PHYS, BLOCK, BLOCK), 1.0, 6.0, ((0, 8), (1, 4)))
    left_env = scatter_about(seeds[1], (PARTITIONS, TERMS, SECTORS, BLOCK, BLOCK), (BLOCK * TERMS) ** -0.5, 0.109375, ((0, 8), (2, 4)))
    right_env = scatter_about(seeds[2], (PARTITIONS, TERMS, SECTORS, BLOCK, BLOCK), BLOCK ** -0.5, 0.5, ((0, 8), (2, 4)))
    local_ops = scatter_about(seeds[3], (TERMS, PHYS, PHYS), PHYS ** -0.5, 3.0)
    targets = draw_targets(jax.random.fold_in(seeds[5], 71), 0)
    return {"wavefunction": wavefunction, "left_env": left_env, "right_env": right_env, "local_ops": local_ops, "targets": targets}


def reference(wavefunction, left_env, right_env, local_ops, targets):
    right_next = jnp.roll(right_env, -1, axis=0)
    choose = (targets[:, :, None] == jnp.arange(SECTORS, dtype=jnp.int32)[None, None, :]).astype(jnp.float32)
    choose = choose.reshape(TERMS, N_SEC, SEC_DEV, SECTORS)

    def one_part(pieces):
        wave_part, left_part, right_part = pieces
        mixed_states = jnp.einsum("wpq,sqab->wspab", local_ops.astype(jnp.float32), wave_part.astype(jnp.float32)).astype(jnp.bfloat16)
        leftpart = jnp.einsum("wsab,wspbc->wspac", left_part.astype(jnp.float32), mixed_states.astype(jnp.float32)).astype(jnp.bfloat16)
        term_blocks = jnp.einsum("wspac,wsdc->wspad", leftpart.astype(jnp.float32), right_part.astype(jnp.float32))
        term_blocks = term_blocks.reshape(TERMS, N_SEC, SEC_DEV, PHYS, BLOCK, BLOCK)
        partial_sums = jnp.einsum("wgst,wgspad->gtpad", choose, term_blocks, precision=lax.Precision.HIGHEST).astype(jnp.bfloat16)
        return jnp.sum(partial_sums.astype(jnp.float32), axis=0).astype(jnp.bfloat16)

    return lax.map(one_part, (wavefunction, left_env, right_next))
```

```python
import functools

import jax
import jax.numpy as jnp
from jax import lax
from jax.experimental import pallas as pl
from jax.experimental.pallas import tpu as pltpu
from jax.sharding import PartitionSpec as P

REACH = 1
MESH = pl.DeviceIdType.MESH
F32 = jnp.float32
BF16 = jnp.bfloat16
FIRST_CUTS = (0, 4, 8)
LAST_CUTS = (0, 2, 4, 6, 8)
PIECES = 2


def plan(sec, terms, block):
    edges = [1 + (terms - 1) * p // PIECES for p in range(PIECES + 1)]
    pieces = list(zip(edges, edges[1:]))
    chunks = []
    for s in reversed(range(sec)):
        cuts = LAST_CUTS if s == 0 else FIRST_CUTS
        cuts = [block * cut // 8 for cut in cuts]
        chunks += [(s, d0, d1) for d0, d1 in zip(cuts, cuts[1:])]
    return chunks, pieces


def joins(n_sec, sec):
    return n_sec == 4 and sec > 1


def kernel(
    all_sectors, ops_hbm, tgt_hbm, psi_hbm, left_ref, right_ref, out_ref,
    ops_ref, tgt_ref, psi_ref, table, marks, lbuf, rbuf, psit, lpt, rm, acc, mid, low_out, high_out, far_out, low_in, high_in, far_in, via_in,
    isem, lsem, rsend, rrecv, ksend, krecv, zsend, zrecv, vrecv, ready,
):
    _, sec, phys, block, _ = psi_hbm.shape
    terms = left_ref.shape[1]
    chunks, pieces = plan(sec, terms, block)
    n_dom, n_sec = lax.axis_size("dom"), lax.axis_size("sec")
    dom, col = lax.axis_index("dom"), lax.axis_index("sec")
    before, after = lax.rem(dom + n_dom - 1, n_dom), lax.rem(dom + 1, n_dom)
    below, above = lax.rem(col + n_sec - 1, n_sec), lax.rem(col + 1, n_sec)
    across = lax.rem(col + n_sec // 2, n_sec)
    peers = (below, above, across)
    first = col * sec
    relay = joins(n_sec, sec)
    low_end, low_mid = col == 0, col == 1
    high_mid, high_end = col == n_sec - 2, col == n_sec - 1

    barrier = pltpu.get_barrier_semaphore()
    pl.semaphore_signal(barrier, inc=1, device_id={"dom": after}, device_id_type=MESH)
    lower = jnp.int32(0)
    for peer in peers:
        lower += (peer < col).astype(jnp.int32)

        @pl.when(peer > col)
        def _():
            pl.semaphore_signal(barrier, inc=1, device_id={"sec": peer}, device_id_type=MESH)

    pl.semaphore_wait(barrier, 1 + lower)

    def r_copy(src, dst, send, recv):
        return pltpu.make_async_remote_copy(
            src_ref=src, dst_ref=dst, send_sem=send, recv_sem=recv, device_id={"dom": before}, device_id_type=MESH,
        )

    right_copies = []
    for c, (s, d0, d1) in enumerate(chunks):
        row = []
        for p, (w0, w1) in enumerate(pieces):
            ws, ds = pl.ds(w0, w1 - w0), pl.ds(d0, d1 - d0)
            row.append(r_copy(right_ref.at[0, ws, s, ds], rbuf.at[s, ws, ds], rsend.at[c, p], rrecv.at[c, p]))
            row[-1].start()
        right_copies.append(row)
    keep_copies = []
    for s in range(sec):
        keep_copies.append(r_copy(right_ref.at[0, 0, s], rbuf.at[s, 0], ksend.at[s], krecv.at[s]))
        keep_copies[-1].start()

    small_copies = [
        pltpu.make_async_copy(psi_hbm, psi_ref, isem.at[0]),
        pltpu.make_async_copy(ops_hbm, ops_ref, isem.at[1]),
        pltpu.make_async_copy(tgt_hbm, tgt_ref, isem.at[2]),
    ]
    for copy in small_copies:
        copy.start()
    left_copies = [pltpu.make_async_copy(left_ref.at[0, :, s], lbuf.at[s], lsem.at[s]) for s in range(sec)]
    for copy in reversed(left_copies):
        copy.start()

    for peer in peers:

        @pl.when(peer < col)
        def _():
            pl.semaphore_signal(ready, inc=1, device_id={"sec": peer}, device_id_type=MESH)

    for copy in small_copies:
        copy.wait()
    for i in range(phys):
        row = ops_ref[i].astype(F32)
        for w in range(terms):
            table[w, i] = jnp.broadcast_to(row[:, w : w + 1], (phys, block))
    for s in range(sec):
        for w in range(1, terms):
            goal = tgt_ref[first + s, w]
            for k, step in enumerate((-REACH, 0, REACH, all_sectors // 2)):
                want = lax.rem(first + s + step + all_sectors, all_sectors)
                marks[s, w, k] = jnp.full((16, block), (goal == want).astype(F32)).astype(BF16)
    for s in range(sec):
        for q in range(phys):
            psit[s, q * block : (q + 1) * block, :] = psi_ref[0, s, q].astype(F32).T.astype(BF16)

    def contract_left(s):
        left_copies[s].wait()

        def left_group(w0, count):
            for v in range(0, count, 2):
                pair = lbuf[s, pl.ds(w0 + v, 2)].reshape(2 * block, block)
                z = lax.dot_general(
                    psit[s], pair, (((1,), (1,)), ((), ())), preferred_element_type=F32
                ).astype(BF16)
                for u in range(2):
                    w = w0 + v + u
                    rows = pl.ds(pl.multiple_of(w * block, block), block)
                    piece = [
                        z[q * block : (q + 1) * block, u * block : (u + 1) * block].reshape(
                            block // 16, 16, block
                        )
                        for q in range(phys)
                    ]
                    for i in range(phys):
                        total = None
                        for q in range(phys):
                            factor = jnp.broadcast_to(table[w, i, q : q + 1, :], (16, block))
                            part = factor.astype(BF16)[None] * piece[q]
                            total = part if total is None else total + part
                        lpt[s, rows, i * block : (i + 1) * block] = total.reshape(block, block)

        def left_quad(j, carry):
            left_group(4 * j, 4)
            return carry

        lax.fori_loop(0, terms // 4, left_quad, 0)
        if terms % 4:
            left_group(terms // 4 * 4, terms % 4)

    contract_left(sec - 1)
    @pl.when(lower < len(peers))
    def _():
        pl.semaphore_wait(ready, len(peers) - lower)


    def z_copy(m, src, dst, where, arrived=None):
        return pltpu.make_async_remote_copy(
            src_ref=src, dst_ref=dst, send_sem=zsend.at[m], recv_sem=(zrecv if arrived is None else arrived).at[m],
            device_id={"sec": where}, device_id_type=MESH,
        )

    def only(condition, action):
        if condition is True:
            action()
        elif condition is not False:
            pl.when(condition)(action)

    if relay:
        for mine, landing in (
            (low_end, high_in), (low_mid, far_in.at[sec - 1]), (high_mid, far_in.at[0]), (high_end, low_in),
        ):

            @pl.when(mine)
            def _():
                landing[...] = jnp.zeros_like(landing)

    z_sent = []
    z_due = []
    via_due = []
    keep_rows = []
    n_msg = 0

    def settle(due, d0, d1, here=False):
        rest = []
        for entry in due:
            if entry[1] < d1 and d0 < entry[2]:
                only(True if here else entry[0], entry[3].wait_recv)
            else:
                rest.append(entry)
        return rest

    def send_on(d0, d1):
        ds = pl.ds(d0, d1 - d0)
        moves = [
            (via_in.at[0, ds], high_out.at[ds], high_in.at[ds], above),
            (via_in.at[1, ds], far_out.at[sec - 1, ds], far_in.at[sec - 1, ds], across),
        ]
        copies = [z_copy(n_msg + j, held, landing, where) for j, (_, held, landing, where) in enumerate(moves)]

        @pl.when(low_mid)
        def _():
            settle(via_up, d0, d1, here=True)
            for (via, held, _, _), copy in zip(moves, copies):
                held[...] = (held[...].astype(F32) + via[...].astype(F32)).astype(BF16)
                copy.start()

        via_up[:] = [entry for entry in via_up if not (entry[1] < d1 and d0 < entry[2])]
        for copy, receiver in zip(copies, (high_mid, high_end)):
            z_sent.append((low_mid, copy))
            z_due.append((receiver, d0, d1, copy))

    via_up = []
    to_send_on = []
    for c, (s, d0, d1) in enumerate(chunks):
        size = d1 - d0
        for p, (w0, w1) in enumerate(pieces):
            right_copies[c][p].wait_recv()
            for w in range(w0, w1):
                right = rbuf[s, w, pl.ds(d0, size)].reshape(size // 16, 16, block)
                column = slice((w - w0) * block, (w - w0 + 1) * block)
                for k in range(4):
                    rm[k * size : (k + 1) * size, column] = (
                        right * marks[s, w, k][None]
                    ).reshape(size, block)
            part = jnp.dot(
                rm[: 4 * size, : (w1 - w0) * block],
                lpt[s, w0 * block : w1 * block, :],
                preferred_element_type=F32,
            )
            if p == 0:
                acc[: 4 * size, :] = part
            else:
                acc[: 4 * size, :] += part
        sums = [acc[k * size : (k + 1) * size, :] for k in range(4)]
        ds = pl.ds(d0, size)
        if relay and s == 0:

            @pl.when(high_mid)
            def _():
                settle(via_due, d0, d1, here=True)
                far_out[s, ds] = (sums[3] + via_in[1, ds].astype(F32)).astype(BF16)
                low_out[ds] = (sums[0] + via_in[0, ds].astype(F32)).astype(BF16)

            @pl.when(col != n_sec - 2)
            def _():
                far_out[s, ds] = sums[3].astype(BF16)
                low_out[ds] = sums[0].astype(BF16)

            via_due = [entry for entry in via_due if not (entry[1] < d1 and d0 < entry[2])]
        else:
            far_out[s, ds] = sums[3].astype(BF16)
            if s == 0:
                low_out[ds] = sums[0].astype(BF16)
        if s == sec - 1:
            high_out[ds] = sums[2].astype(BF16)

        messages = [("far", far_out.at[s, ds], far_in.at[s, ds], across)]
        if s == 0:
            messages.append(("low", low_out.at[ds], low_in.at[ds], below))
        if s == sec - 1:
            messages.append(("high", high_out.at[ds], high_in.at[ds], above))
        for kind, src, landing, where in messages:
            copy = z_copy(n_msg, src, landing, where)
            straight, due = True, True
            if relay and s in (0, sec - 1):
                rising = s == 0
                end, mid_col = (low_end, low_mid) if rising else (high_end, high_mid)
                step = above if rising else below
                via = z_copy(n_msg, src, via_in.at[0 if kind == "far" else 1, ds], step, vrecv)
                only(end, via.start)
                (via_up if rising else via_due).append((mid_col, d0, d1, via))
                if rising:
                    straight = col != 0
                    due = (col != n_sec - 2) if kind == "far" else (col != n_sec - 1)
                    z_sent.append((True, copy))
                else:
                    straight = jnp.logical_and(col != 1, col != n_sec - 1)
                    due = lax.rem(col, 2) == 0 if kind == "far" else lax.rem(col, 2) == 1
                    z_sent.append((col != 1, copy))
            else:
                z_sent.append((True, copy))
            only(straight, copy.start)
            z_due.append((due, d0, d1, copy))
            n_msg += 1
        if relay and s == 0:
            to_send_on.append((d0, d1))
            if len(to_send_on) > 1:
                send_on(*to_send_on.pop(0))
                n_msg += 2

        if s > 0 and d0 == 0:
            contract_left(s - 1)
        if s < sec - 1:
            mid[s + 1, ds] += sums[2]
            mid[s, ds] += sums[1]
        else:
            mid[s, ds] = sums[1]
        if s > 0:
            mid[s - 1, ds] = sums[0]
        else:
            keep_rows.append((d0, d1))

    for s in reversed(range(sec)):
        keep_copies[s].wait_recv()
        mid[s] += jnp.dot(rbuf[s, 0], lpt[s, :block, :], preferred_element_type=F32)
    for rows in to_send_on:
        send_on(*rows)
        n_msg += 2
    for d0, d1 in keep_rows:
        z_due = settle(z_due, d0, d1)
        ds = pl.ds(d0, d1 - d0)
        for t in range(sec):
            total = mid[t, ds] + far_in[t, ds].astype(F32)
            if t == 0:
                total = total + high_in[ds].astype(F32)
            if t == sec - 1:
                total = total + low_in[ds].astype(F32)
            for i in range(phys):
                out_ref[0, t, i, :, d0:d1] = total[:, i * block : (i + 1) * block].T.astype(BF16)
    for row in right_copies + [keep_copies]:
        for copy in row:
            copy.wait_send()
    for senders, copy in z_sent:
        only(senders, copy.wait_send)


def local(wavefunction, left_env, right_env, local_ops, targets):
    _, sec, phys, block, _ = wavefunction.shape
    terms = left_env.shape[1]
    wide = phys * block
    chunks, pieces = plan(sec, terms, block)
    n_msg = sum(1 + (s == 0) + (s == sec - 1) for s, _, _ in chunks)
    if joins(lax.axis_size("sec"), sec):
        n_msg += sum(2 * (s == 0) for s, _, _ in chunks)
    longest = max(w1 - w0 for w0, w1 in pieces)
    return pl.pallas_call(
        functools.partial(kernel, targets.shape[1]),
        out_shape=pltpu.VMEM(wavefunction.shape, BF16),
        in_specs=[
            pl.BlockSpec(memory_space=pl.ANY),
            pl.BlockSpec(memory_space=pl.ANY),
            pl.BlockSpec(memory_space=pl.ANY),
            pl.BlockSpec(memory_space=pl.ANY),
            pl.BlockSpec(memory_space=pl.ANY),
        ],
        out_specs=pl.BlockSpec(memory_space=pltpu.VMEM),
        scratch_shapes=[
            pltpu.VMEM((phys, phys, terms), BF16),
            pltpu.SMEM(targets.shape[::-1], jnp.int32),
            pltpu.VMEM(wavefunction.shape, BF16),
            pltpu.VMEM((terms, phys, phys, block), F32),
            pltpu.VMEM((sec, terms, 4, 16, block), BF16),
            pltpu.VMEM((sec, terms, block, block), BF16),
            pltpu.VMEM((sec, terms, block, block), BF16),
            pltpu.VMEM((sec, wide, block), BF16),
            pltpu.VMEM((sec, terms * block, wide), BF16),
            pltpu.VMEM((4 * block, longest * block), BF16),
            pltpu.VMEM((4 * block, wide), F32),
            pltpu.VMEM((sec, block, wide), F32),
            pltpu.VMEM((block, wide), BF16),
            pltpu.VMEM((block, wide), BF16),
            pltpu.VMEM((sec, block, wide), BF16),
            pltpu.VMEM((block, wide), BF16),
            pltpu.VMEM((block, wide), BF16),
            pltpu.VMEM((sec, block, wide), BF16),
            pltpu.VMEM((2, block, wide), BF16),
            pltpu.SemaphoreType.DMA((3,)),
            pltpu.SemaphoreType.DMA((sec,)),
            pltpu.SemaphoreType.DMA((len(chunks), len(pieces))),
            pltpu.SemaphoreType.DMA((len(chunks), len(pieces))),
            pltpu.SemaphoreType.DMA((sec,)),
            pltpu.SemaphoreType.DMA((sec,)),
            pltpu.SemaphoreType.DMA((n_msg,)),
            pltpu.SemaphoreType.DMA((n_msg,)),
            pltpu.SemaphoreType.DMA((n_msg,)),
            pltpu.SemaphoreType.REGULAR,
        ],
        compiler_params=pltpu.CompilerParams(collective_id=0, has_side_effects=True),
    )(local_ops.transpose(1, 2, 0), targets.T, wavefunction, left_env, right_env)


def solution(mesh):
    return jax.shard_map(
        local,
        mesh=mesh,
        in_specs=(
            P("dom", "sec", None, None, None),
            P("dom", None, "sec", None, None),
            P("dom", None, "sec", None, None),
            P(),
            P(),
        ),
        out_specs=P("dom", "sec", None, None, None),
        check_vma=False,
    )
```

```python
import functools

import jax
import jax.numpy as jnp
from jax import lax
from jax.experimental import pallas as pl
from jax.experimental.pallas import tpu as pltpu
from jax.sharding import PartitionSpec as P

REACH = 1
MESH = pl.DeviceIdType.MESH
F32 = jnp.float32
BF16 = jnp.bfloat16
FIRST_CUTS = (0, 4, 8)
LAST_CUTS = (0, 4, 6, 7, 8)
PIECES = (3, 5)


def plan(sec, terms, block):
    chunks = []
    for s in reversed(range(sec)):
        cuts = LAST_CUTS if s == 0 else FIRST_CUTS
        cuts = [block * cut // 8 for cut in cuts]
        chunks += [(s, d0, d1) for d0, d1 in zip(cuts, cuts[1:])]
    edges = [1 + (terms - 1) * cut // PIECES[-1] for cut in (0,) + PIECES]
    pieces = [[(1, terms)] for _ in chunks[1:]] + [list(zip(edges, edges[1:]))]
    return chunks, pieces


def joins(n_sec, sec):
    return n_sec == 4 and sec > 1


def kernel(
    all_sectors, ops_hbm, tgt_hbm, psi_hbm, left_ref, right_ref, out_ref,
    ops_ref, tgt_ref, psi_ref, table, marks, lbuf, rbuf, psit, lpt, rm, acc, mid, low_out, high_out, far_out, low_in, high_in, far_in, via_in, fin,
    isem, lsem, rsend, rrecv, ksend, krecv, zsend, zrecv, vrecv, ready,
):
    _, sec, phys, block, _ = psi_hbm.shape
    terms = left_ref.shape[1]
    chunks, pieces = plan(sec, terms, block)
    n_dom, n_sec = lax.axis_size("dom"), lax.axis_size("sec")
    dom, col = lax.axis_index("dom"), lax.axis_index("sec")
    before, after = lax.rem(dom + n_dom - 1, n_dom), lax.rem(dom + 1, n_dom)
    below, above = lax.rem(col + n_sec - 1, n_sec), lax.rem(col + 1, n_sec)
    across = lax.rem(col + n_sec // 2, n_sec)
    peers = (below, above, across)
    first = col * sec
    relay = joins(n_sec, sec)
    low_end, low_mid = col == 0, col == 1
    high_mid, high_end = col == n_sec - 2, col == n_sec - 1

    barrier = pltpu.get_barrier_semaphore()
    pl.semaphore_signal(barrier, inc=1, device_id={"dom": after}, device_id_type=MESH)
    lower = jnp.int32(0)
    for peer in peers:
        lower += (peer < col).astype(jnp.int32)

        @pl.when(peer > col)
        def _():
            pl.semaphore_signal(barrier, inc=1, device_id={"sec": peer}, device_id_type=MESH)

    small_copies = [
        pltpu.make_async_copy(psi_hbm, psi_ref, isem.at[0]),
        pltpu.make_async_copy(ops_hbm, ops_ref, isem.at[1]),
        pltpu.make_async_copy(tgt_hbm, tgt_ref, isem.at[2]),
    ]
    for copy in small_copies:
        copy.start()
    left_copies = [pltpu.make_async_copy(left_ref.at[0, :, s], lbuf.at[s], lsem.at[s]) for s in range(sec)]
    for copy in reversed(left_copies):
        copy.start()

    def prepare():
        for copy in small_copies:
            copy.wait()
        for i in range(phys):
            row = ops_ref[i].astype(F32)
            for w in range(terms):
                table[w, i] = jnp.broadcast_to(row[:, w : w + 1], (phys, block))
        for s in range(sec):
            for w in range(1, terms):
                goal = tgt_ref[first + s, w]
                for k, step in enumerate((-REACH, 0, REACH, all_sectors // 2)):
                    want = lax.rem(first + s + step + all_sectors, all_sectors)
                    marks[s, w, k] = jnp.full((16, block), (goal == want).astype(F32)).astype(BF16)
        for s in range(sec):
            for q in range(phys):
                psit[s, q * block : (q + 1) * block, :] = psi_ref[0, s, q].astype(F32).T.astype(BF16)

    pl.when(dom == 0)(prepare)
    pl.semaphore_wait(barrier, 1 + lower)

    def r_copy(src, dst, send, recv):
        return pltpu.make_async_remote_copy(
            src_ref=src, dst_ref=dst, send_sem=send, recv_sem=recv, device_id={"dom": before}, device_id_type=MESH,
        )

    right_copies = []
    for c, (s, d0, d1) in enumerate(chunks):
        row = []
        for p, (w0, w1) in enumerate(pieces[c]):
            ws, ds = pl.ds(w0, w1 - w0), pl.ds(d0, d1 - d0)
            row.append(r_copy(right_ref.at[0, ws, s, ds], rbuf.at[s, ws, ds], rsend.at[c, p], rrecv.at[c, p]))
            row[-1].start()
        right_copies.append(row)
    keep_copies = []
    for s in range(sec):
        keep_copies.append(r_copy(right_ref.at[0, 0, s], rbuf.at[s, 0], ksend.at[s], krecv.at[s]))
        keep_copies[-1].start()

    for peer in peers:

        @pl.when(peer < col)
        def _():
            pl.semaphore_signal(ready, inc=1, device_id={"sec": peer}, device_id_type=MESH)

    pl.when(dom != 0)(prepare)

    def contract_left(s):
        left_copies[s].wait()

        def left_group(w0, count):
            for v in range(0, count, 2):
                pair = lbuf[s, pl.ds(w0 + v, 2)].reshape(2 * block, block)
                z = lax.dot_general(
                    psit[s], pair, (((1,), (1,)), ((), ())), preferred_element_type=F32
                ).astype(BF16)
                for u in range(2):
                    w = w0 + v + u
                    rows = pl.ds(pl.multiple_of(w * block, block), block)
                    piece = [
                        z[q * block : (q + 1) * block, u * block : (u + 1) * block].reshape(
                            block // 16, 16, block
                        )
                        for q in range(phys)
                    ]
                    for i in range(phys):
                        total = None
                        for q in range(phys):
                            factor = jnp.broadcast_to(table[w, i, q : q + 1, :], (16, block))
                            part = factor.astype(BF16)[None] * piece[q]
                            total = part if total is None else total + part
                        lpt[s, rows, i * block : (i + 1) * block] = total.reshape(block, block)

        def left_quad(j, carry):
            left_group(4 * j, 4)
            return carry

        lax.fori_loop(0, terms // 4, left_quad, 0)
        if terms % 4:
            left_group(terms // 4 * 4, terms % 4)

    contract_left(sec - 1)
    @pl.when(lower < len(peers))
    def _():
        pl.semaphore_wait(ready, len(peers) - lower)


    def z_copy(m, src, dst, where, arrived=None):
        return pltpu.make_async_remote_copy(
            src_ref=src, dst_ref=dst, send_sem=zsend.at[m], recv_sem=(zrecv if arrived is None else arrived).at[m],
            device_id={"sec": where}, device_id_type=MESH,
        )

    def only(condition, action):
        if condition is True:
            action()
        elif condition is not False:
            pl.when(condition)(action)

    if relay:
        for mine, landing in (
            (low_end, high_in), (low_mid, far_in.at[sec - 1]), (high_mid, far_in.at[0]), (high_end, low_in),
        ):

            @pl.when(mine)
            def _():
                landing[...] = jnp.zeros_like(landing)

    z_sent = []
    z_due = []
    via_due = []
    keep_rows = []
    n_msg = 0

    def settle(due, d0, d1, here=False):
        rest = []
        for entry in due:
            if entry[1] < d1 and d0 < entry[2]:
                only(True if here else entry[0], entry[3].wait_recv)
            else:
                rest.append(entry)
        return rest

    def send_on(d0, d1):
        ds = pl.ds(d0, d1 - d0)
        moves = [
            (via_in.at[0, ds], high_out.at[ds], high_in.at[ds], above),
            (via_in.at[1, ds], far_out.at[sec - 1, ds], far_in.at[sec - 1, ds], across),
        ]
        copies = [z_copy(n_msg + j, held, landing, where) for j, (_, held, landing, where) in enumerate(moves)]

        @pl.when(low_mid)
        def _():
            settle(via_up, d0, d1, here=True)
            for (via, held, _, _), copy in zip(moves, copies):
                held[...] = (held[...].astype(F32) + via[...].astype(F32)).astype(BF16)
                copy.start()

        via_up[:] = [entry for entry in via_up if not (entry[1] < d1 and d0 < entry[2])]
        for copy, receiver in zip(copies, (high_mid, high_end)):
            z_sent.append((low_mid, copy))
            z_due.append((receiver, d0, d1, copy))

    via_up = []
    to_send_on = []
    for c, (s, d0, d1) in enumerate(chunks):
        size = d1 - d0
        for p, (w0, w1) in enumerate(pieces[c]):
            right_copies[c][p].wait_recv()
            for w in range(w0, w1):
                right = rbuf[s, w, pl.ds(d0, size)].reshape(size // 16, 16, block)
                column = slice((w - w0) * block, (w - w0 + 1) * block)
                for k in range(4):
                    rm[k * size : (k + 1) * size, column] = (
                        right * marks[s, w, k][None]
                    ).reshape(size, block)
            part = jnp.dot(
                rm[: 4 * size, : (w1 - w0) * block],
                lpt[s, w0 * block : w1 * block, :],
                preferred_element_type=F32,
            )
            if p == 0:
                acc[: 4 * size, :] = part
            else:
                acc[: 4 * size, :] += part
        sums = [acc[k * size : (k + 1) * size, :] for k in range(4)]
        ds = pl.ds(d0, size)
        if relay and s == 0:

            @pl.when(high_mid)
            def _():
                settle(via_due, d0, d1, here=True)
                far_out[s, ds] = (sums[3] + via_in[1, ds].astype(F32)).astype(BF16)
                low_out[ds] = (sums[0] + via_in[0, ds].astype(F32)).astype(BF16)

            @pl.when(col != n_sec - 2)
            def _():
                far_out[s, ds] = sums[3].astype(BF16)
                low_out[ds] = sums[0].astype(BF16)

            via_due = [entry for entry in via_due if not (entry[1] < d1 and d0 < entry[2])]
        else:
            far_out[s, ds] = sums[3].astype(BF16)
            if s == 0:
                low_out[ds] = sums[0].astype(BF16)
        if s == sec - 1:
            high_out[ds] = sums[2].astype(BF16)

        messages = [("far", far_out.at[s, ds], far_in.at[s, ds], across)]
        if s == 0:
            messages.append(("low", low_out.at[ds], low_in.at[ds], below))
        if s == sec - 1:
            messages.append(("high", high_out.at[ds], high_in.at[ds], above))
        for kind, src, landing, where in messages:
            copy = z_copy(n_msg, src, landing, where)
            straight, due = True, True
            if relay and s in (0, sec - 1):
                rising = s == 0
                end, mid_col = (low_end, low_mid) if rising else (high_end, high_mid)
                step = above if rising else below
                via = z_copy(n_msg, src, via_in.at[0 if kind == "far" else 1, ds], step, vrecv)
                only(end, via.start)
                (via_up if rising else via_due).append((mid_col, d0, d1, via))
                if rising:
                    straight = col != 0
                    due = (col != n_sec - 2) if kind == "far" else (col != n_sec - 1)
                    z_sent.append((True, copy))
                else:
                    straight = jnp.logical_and(col != 1, col != n_sec - 1)
                    due = lax.rem(col, 2) == 0 if kind == "far" else lax.rem(col, 2) == 1
                    z_sent.append((col != 1, copy))
            else:
                z_sent.append((True, copy))
            only(straight, copy.start)
            z_due.append((due, d0, d1, copy))
            n_msg += 1
        if relay and s == 0:
            to_send_on.append((d0, d1))
            if len(to_send_on) > 1:
                send_on(*to_send_on.pop(0))
                n_msg += 2

        if s > 0 and d0 == 0:
            contract_left(s - 1)
        if s < sec - 1:
            mid[s + 1, ds] += sums[2]
            mid[s, ds] += sums[1]
        else:
            mid[s, ds] = sums[1]
        if s > 0:
            mid[s - 1, ds] = sums[0]
        else:
            keep_rows.append((d0, d1))

    for s in reversed(range(sec)):
        keep_copies[s].wait_recv()
        mid[s] += jnp.dot(rbuf[s, 0], lpt[s, :block, :], preferred_element_type=F32)
    for rows in to_send_on:
        send_on(*rows)
        n_msg += 2
    for d0, d1 in keep_rows:
        z_due = settle(z_due, d0, d1)
        ds = pl.ds(d0, d1 - d0)
        for t in range(sec):
            total = mid[t, ds] + far_in[t, ds].astype(F32)
            if t == 0:
                total = total + high_in[ds].astype(F32)
            if t == sec - 1:
                total = total + low_in[ds].astype(F32)
            fin[t, ds] = total.astype(BF16)
    for t in range(sec):
        for i in range(phys):
            out_ref[0, t, i] = fin[t, :, i * block : (i + 1) * block].T.astype(BF16)
    for row in right_copies + [keep_copies]:
        for copy in row:
            copy.wait_send()
    for senders, copy in z_sent:
        only(senders, copy.wait_send)


def local(wavefunction, left_env, right_env, local_ops, targets):
    _, sec, phys, block, _ = wavefunction.shape
    terms = left_env.shape[1]
    wide = phys * block
    chunks, pieces = plan(sec, terms, block)
    n_msg = sum(1 + (s == 0) + (s == sec - 1) for s, _, _ in chunks)
    if joins(lax.axis_size("sec"), sec):
        n_msg += sum(2 * (s == 0) for s, _, _ in chunks)
    longest = max(w1 - w0 for row in pieces for w0, w1 in row)
    return pl.pallas_call(
        functools.partial(kernel, targets.shape[1]),
        out_shape=pltpu.VMEM(wavefunction.shape, BF16),
        in_specs=[
            pl.BlockSpec(memory_space=pl.ANY),
            pl.BlockSpec(memory_space=pl.ANY),
            pl.BlockSpec(memory_space=pl.ANY),
            pl.BlockSpec(memory_space=pl.ANY),
            pl.BlockSpec(memory_space=pl.ANY),
        ],
        out_specs=pl.BlockSpec(memory_space=pltpu.VMEM),
        scratch_shapes=[
            pltpu.VMEM((phys, phys, terms), BF16),
            pltpu.SMEM(targets.shape[::-1], jnp.int32),
            pltpu.VMEM(wavefunction.shape, BF16),
            pltpu.VMEM((terms, phys, phys, block), F32),
            pltpu.VMEM((sec, terms, 4, 16, block), BF16),
            pltpu.VMEM((sec, terms, block, block), BF16),
            pltpu.VMEM((sec, terms, block, block), BF16),
            pltpu.VMEM((sec, wide, block), BF16),
            pltpu.VMEM((sec, terms * block, wide), BF16),
            pltpu.VMEM((4 * block, longest * block), BF16),
            pltpu.VMEM((4 * block, wide), F32),
            pltpu.VMEM((sec, block, wide), F32),
            pltpu.VMEM((block, wide), BF16),
            pltpu.VMEM((block, wide), BF16),
            pltpu.VMEM((sec, block, wide), BF16),
            pltpu.VMEM((block, wide), BF16),
            pltpu.VMEM((block, wide), BF16),
            pltpu.VMEM((sec, block, wide), BF16),
            pltpu.VMEM((2, block, wide), BF16),
            pltpu.VMEM((sec, block, wide), BF16),
            pltpu.SemaphoreType.DMA((3,)),
            pltpu.SemaphoreType.DMA((sec,)),
            pltpu.SemaphoreType.DMA((len(chunks), len(PIECES))),
            pltpu.SemaphoreType.DMA((len(chunks), len(PIECES))),
            pltpu.SemaphoreType.DMA((sec,)),
            pltpu.SemaphoreType.DMA((sec,)),
            pltpu.SemaphoreType.DMA((n_msg,)),
            pltpu.SemaphoreType.DMA((n_msg,)),
            pltpu.SemaphoreType.DMA((n_msg,)),
            pltpu.SemaphoreType.REGULAR,
        ],
        compiler_params=pltpu.CompilerParams(collective_id=0, has_side_effects=True),
    )(local_ops.transpose(1, 2, 0), targets.T, wavefunction, left_env, right_env)


def solution(mesh):
    return jax.shard_map(
        local,
        mesh=mesh,
        in_specs=(
            P("dom", "sec", None, None, None),
            P("dom", None, "sec", None, None),
            P("dom", None, "sec", None, None),
            P(),
            P(),
        ),
        out_specs=P("dom", "sec", None, None, None),
        check_vma=False,
    )
```

```python
import functools

import jax
import jax.numpy as jnp
from jax import lax
from jax.experimental import pallas as pl
from jax.experimental.pallas import tpu as pltpu
from jax.sharding import PartitionSpec as P

REACH = 1
MESH = pl.DeviceIdType.MESH
F32 = jnp.float32
BF16 = jnp.bfloat16
FIRST_CUTS = (0, 4, 8)
LAST_CUTS = (0, 4, 6, 7, 8)
PIECES = (3, 5)


def plan(sec, terms, block):
    chunks = []
    for s in reversed(range(sec)):
        cuts = LAST_CUTS if s == 0 else FIRST_CUTS
        cuts = [block * cut // 8 for cut in cuts]
        chunks += [(s, d0, d1) for d0, d1 in zip(cuts, cuts[1:])]
    edges = [1 + (terms - 1) * cut // PIECES[-1] for cut in (0,) + PIECES]
    pieces = [[(1, terms)] for _ in chunks[1:]] + [list(zip(edges, edges[1:]))]
    return chunks, pieces


def joins(n_sec, sec):
    return n_sec == 4 and sec > 1


def kernel(
    all_sectors, ops_hbm, tgt_hbm, psi_hbm, left_ref, right_ref, out_ref,
    ops_ref, tgt_ref, psi_ref, table, marks, lbuf, rbuf, psit, lpt, rm, acc, mid, low_out, high_out, far_out, low_in, high_in, far_in, via_in, fin,
    isem, lsem, rsend, rrecv, ksend, krecv, zsend, zrecv, vrecv, ready,
):
    _, sec, phys, block, _ = psi_hbm.shape
    terms = left_ref.shape[1]
    chunks, pieces = plan(sec, terms, block)
    n_dom, n_sec = lax.axis_size("dom"), lax.axis_size("sec")
    dom, col = lax.axis_index("dom"), lax.axis_index("sec")
    before, after = lax.rem(dom + n_dom - 1, n_dom), lax.rem(dom + 1, n_dom)
    below, above = lax.rem(col + n_sec - 1, n_sec), lax.rem(col + 1, n_sec)
    across = lax.rem(col + n_sec // 2, n_sec)
    peers = (below, above, across)
    first = col * sec
    relay = joins(n_sec, sec)
    low_end, low_mid = col == 0, col == 1
    high_mid, high_end = col == n_sec - 2, col == n_sec - 1

    barrier = pltpu.get_barrier_semaphore()
    pl.semaphore_signal(barrier, inc=1, device_id={"dom": after}, device_id_type=MESH)
    lower = jnp.int32(0)
    for peer in peers:
        lower += (peer < col).astype(jnp.int32)

        @pl.when(peer > col)
        def _():
            pl.semaphore_signal(barrier, inc=1, device_id={"sec": peer}, device_id_type=MESH)

    small_copies = [
        pltpu.make_async_copy(psi_hbm, psi_ref, isem.at[0]),
        pltpu.make_async_copy(ops_hbm, ops_ref, isem.at[1]),
        pltpu.make_async_copy(tgt_hbm, tgt_ref, isem.at[2]),
    ]
    for copy in small_copies:
        copy.start()
    left_copies = [pltpu.make_async_copy(left_ref.at[0, :, s], lbuf.at[s], lsem.at[s]) for s in range(sec)]
    for copy in reversed(left_copies):
        copy.start()

    def prepare():
        for copy in small_copies:
            copy.wait()
        for i in range(phys):
            row = ops_ref[i].astype(F32)
            for w in range(terms):
                table[w, i] = jnp.broadcast_to(row[:, w : w + 1], (phys, block))
        for s in range(sec):
            for w in range(1, terms):
                goal = tgt_ref[first + s, w]
                for k, step in enumerate((-REACH, 0, REACH, all_sectors // 2)):
                    want = lax.rem(first + s + step + all_sectors, all_sectors)
                    marks[s, w, k] = jnp.full((16, block), (goal == want).astype(F32)).astype(BF16)
        for s in range(sec):
            for q in range(phys):
                psit[s, q * block : (q + 1) * block, :] = psi_ref[0, s, q].astype(F32).T.astype(BF16)

    pl.when(dom == 0)(prepare)
    pl.semaphore_wait(barrier, 1 + lower)

    def r_copy(src, dst, send, recv):
        return pltpu.make_async_remote_copy(
            src_ref=src, dst_ref=dst, send_sem=send, recv_sem=recv, device_id={"dom": before}, device_id_type=MESH,
        )

    right_copies = []
    for c, (s, d0, d1) in enumerate(chunks):
        row = []
        for p, (w0, w1) in enumerate(pieces[c]):
            ws, ds = pl.ds(w0, w1 - w0), pl.ds(d0, d1 - d0)
            row.append(r_copy(right_ref.at[0, ws, s, ds], rbuf.at[s, ws, ds], rsend.at[c, p], rrecv.at[c, p]))
            row[-1].start()
        right_copies.append(row)
    keep_copies = []
    for s in range(sec):
        keep_copies.append(r_copy(right_ref.at[0, 0, s], rbuf.at[s, 0], ksend.at[s], krecv.at[s]))
        keep_copies[-1].start()

    for peer in peers:

        @pl.when(peer < col)
        def _():
            pl.semaphore_signal(ready, inc=1, device_id={"sec": peer}, device_id_type=MESH)

    pl.when(dom != 0)(prepare)

    def contract_left(s):
        left_copies[s].wait()

        def left_group(w0, count):
            for v in range(0, count, 2):
                pair = lbuf[s, pl.ds(w0 + v, 2)].reshape(2 * block, block)
                z = lax.dot_general(
                    psit[s], pair, (((1,), (1,)), ((), ())), preferred_element_type=F32
                ).astype(BF16)
                for u in range(2):
                    w = w0 + v + u
                    rows = pl.ds(pl.multiple_of(w * block, block), block)
                    piece = [
                        z[q * block : (q + 1) * block, u * block : (u + 1) * block].reshape(
                            block // 16, 16, block
                        )
                        for q in range(phys)
                    ]
                    for i in range(phys):
                        total = None
                        for q in range(phys):
                            factor = jnp.broadcast_to(table[w, i, q : q + 1, :], (16, block))
                            part = factor.astype(BF16)[None] * piece[q]
                            total = part if total is None else total + part
                        lpt[s, rows, i * block : (i + 1) * block] = total.reshape(block, block)

        def left_quad(j, carry):
            left_group(4 * j, 4)
            return carry

        lax.fori_loop(0, terms // 4, left_quad, 0)
        if terms % 4:
            left_group(terms // 4 * 4, terms % 4)

    contract_left(sec - 1)
    @pl.when(lower < len(peers))
    def _():
        pl.semaphore_wait(ready, len(peers) - lower)


    def z_copy(m, src, dst, where, arrived=None):
        return pltpu.make_async_remote_copy(
            src_ref=src, dst_ref=dst, send_sem=zsend.at[m], recv_sem=(zrecv if arrived is None else arrived).at[m],
            device_id={"sec": where}, device_id_type=MESH,
        )

    def only(condition, action):
        if condition is True:
            action()
        elif condition is not False:
            pl.when(condition)(action)

    if relay:
        for mine, landing in (
            (low_end, high_in), (low_mid, far_in.at[sec - 1]), (high_mid, far_in.at[0]), (high_end, low_in),
        ):

            @pl.when(mine)
            def _():
                landing[...] = jnp.zeros_like(landing)

    z_sent = []
    z_due = []
    via_due = []
    keep_rows = []
    n_msg = 0

    def settle(due, d0, d1, here=False):
        rest = []
        for entry in due:
            if entry[1] < d1 and d0 < entry[2]:
                only(True if here else entry[0], entry[3].wait_recv)
            else:
                rest.append(entry)
        return rest

    def send_on(d0, d1):
        ds = pl.ds(d0, d1 - d0)
        moves = [
            (via_in.at[0, ds], high_out.at[ds], high_in.at[ds], above),
            (via_in.at[1, ds], far_out.at[sec - 1, ds], far_in.at[sec - 1, ds], across),
        ]
        copies = [z_copy(n_msg + j, held, landing, where) for j, (_, held, landing, where) in enumerate(moves)]

        @pl.when(low_mid)
        def _():
            settle(via_up, d0, d1, here=True)
            for (via, held, _, _), copy in zip(moves, copies):
                held[...] = (held[...].astype(F32) + via[...].astype(F32)).astype(BF16)
                copy.start()

        via_up[:] = [entry for entry in via_up if not (entry[1] < d1 and d0 < entry[2])]
        for copy, receiver in zip(copies, (high_mid, high_end)):
            z_sent.append((low_mid, copy))
            z_due.append((receiver, d0, d1, copy))

    via_up = []
    to_send_on = []
    for c, (s, d0, d1) in enumerate(chunks):
        size = d1 - d0
        for p, (w0, w1) in enumerate(pieces[c]):
            right_copies[c][p].wait_recv()
            for w in range(w0, w1):
                right = rbuf[s, w, pl.ds(d0, size)].reshape(size // 16, 16, block)
                column = slice((w - w0) * block, (w - w0 + 1) * block)
                for k in range(4):
                    rm[k * size : (k + 1) * size, column] = (
                        right * marks[s, w, k][None]
                    ).reshape(size, block)
            part = jnp.dot(
                rm[: 4 * size, : (w1 - w0) * block],
                lpt[s, w0 * block : w1 * block, :],
                preferred_element_type=F32,
            )
            if p == 0:
                acc[: 4 * size, :] = part
            else:
                acc[: 4 * size, :] += part
        sums = [acc[k * size : (k + 1) * size, :] for k in range(4)]
        ds = pl.ds(d0, size)
        if relay and s == 0:

            @pl.when(high_mid)
            def _():
                settle(via_due, d0, d1, here=True)
                far_out[s, ds] = (sums[3] + via_in[1, ds].astype(F32)).astype(BF16)
                low_out[ds] = (sums[0] + via_in[0, ds].astype(F32)).astype(BF16)

            @pl.when(col != n_sec - 2)
            def _():
                far_out[s, ds] = sums[3].astype(BF16)
                low_out[ds] = sums[0].astype(BF16)

            via_due = [entry for entry in via_due if not (entry[1] < d1 and d0 < entry[2])]
        else:
            far_out[s, ds] = sums[3].astype(BF16)
            if s == 0:
                low_out[ds] = sums[0].astype(BF16)
        if s == sec - 1:
            high_out[ds] = sums[2].astype(BF16)

        messages = [("far", far_out.at[s, ds], far_in.at[s, ds], across)]
        if s == 0:
            messages.append(("low", low_out.at[ds], low_in.at[ds], below))
        if s == sec - 1:
            messages.append(("high", high_out.at[ds], high_in.at[ds], above))
        for kind, src, landing, where in messages:
            copy = z_copy(n_msg, src, landing, where)
            straight, due = True, True
            if relay and s in (0, sec - 1):
                rising = s == 0
                end, mid_col = (low_end, low_mid) if rising else (high_end, high_mid)
                step = above if rising else below
                via = z_copy(n_msg, src, via_in.at[0 if kind == "far" else 1, ds], step, vrecv)
                only(end, via.start)
                (via_up if rising else via_due).append((mid_col, d0, d1, via))
                if rising:
                    straight = col != 0
                    due = (col != n_sec - 2) if kind == "far" else (col != n_sec - 1)
                    z_sent.append((True, copy))
                else:
                    straight = jnp.logical_and(col != 1, col != n_sec - 1)
                    due = lax.rem(col, 2) == 0 if kind == "far" else lax.rem(col, 2) == 1
                    z_sent.append((col != 1, copy))
            else:
                z_sent.append((True, copy))
            only(straight, copy.start)
            z_due.append((due, d0, d1, copy))
            n_msg += 1
        if relay and s == 0:
            to_send_on.append((d0, d1))
            if len(to_send_on) > 1:
                send_on(*to_send_on.pop(0))
                n_msg += 2

        if s > 0 and d0 == 0:
            contract_left(s - 1)
        if s < sec - 1:
            mid[s + 1, ds] += sums[2]
            mid[s, ds] += sums[1]
        else:
            mid[s, ds] = sums[1]
        if s > 0:
            mid[s - 1, ds] = sums[0]
        else:
            keep_rows.append((d0, d1))

    for s in reversed(range(sec)):
        keep_copies[s].wait_recv()
        mid[s] += jnp.dot(rbuf[s, 0], lpt[s, :block, :], preferred_element_type=F32)
    for rows in to_send_on:
        send_on(*rows)
        n_msg += 2
    for d0, d1 in keep_rows:
        if d1 == block:
            for row in right_copies + [keep_copies]:
                for copy in row:
                    copy.wait_send()
            for senders, copy in z_sent:
                only(senders, copy.wait_send)
        z_due = settle(z_due, d0, d1)
        ds = pl.ds(d0, d1 - d0)
        for t in range(sec):
            total = mid[t, ds] + far_in[t, ds].astype(F32)
            if t == 0:
                total = total + high_in[ds].astype(F32)
            if t == sec - 1:
                total = total + low_in[ds].astype(F32)
            fin[t, ds] = total.astype(BF16)
    for t in range(sec):
        for i in range(phys):
            out_ref[0, t, i] = fin[t, :, i * block : (i + 1) * block].T.astype(BF16)


def local(wavefunction, left_env, right_env, local_ops, targets):
    _, sec, phys, block, _ = wavefunction.shape
    terms = left_env.shape[1]
    wide = phys * block
    chunks, pieces = plan(sec, terms, block)
    n_msg = sum(1 + (s == 0) + (s == sec - 1) for s, _, _ in chunks)
    if joins(lax.axis_size("sec"), sec):
        n_msg += sum(2 * (s == 0) for s, _, _ in chunks)
    longest = max(w1 - w0 for row in pieces for w0, w1 in row)
    return pl.pallas_call(
        functools.partial(kernel, targets.shape[1]),
        out_shape=pltpu.VMEM(wavefunction.shape, BF16),
        in_specs=[
            pl.BlockSpec(memory_space=pl.ANY),
            pl.BlockSpec(memory_space=pl.ANY),
            pl.BlockSpec(memory_space=pl.ANY),
            pl.BlockSpec(memory_space=pl.ANY),
            pl.BlockSpec(memory_space=pl.ANY),
        ],
        out_specs=pl.BlockSpec(memory_space=pltpu.VMEM),
        scratch_shapes=[
            pltpu.VMEM((phys, phys, terms), BF16),
            pltpu.SMEM(targets.shape[::-1], jnp.int32),
            pltpu.VMEM(wavefunction.shape, BF16),
            pltpu.VMEM((terms, phys, phys, block), F32),
            pltpu.VMEM((sec, terms, 4, 16, block), BF16),
            pltpu.VMEM((sec, terms, block, block), BF16),
            pltpu.VMEM((sec, terms, block, block), BF16),
            pltpu.VMEM((sec, wide, block), BF16),
            pltpu.VMEM((sec, terms * block, wide), BF16),
            pltpu.VMEM((4 * block, longest * block), BF16),
            pltpu.VMEM((4 * block, wide), F32),
            pltpu.VMEM((sec, block, wide), F32),
            pltpu.VMEM((block, wide), BF16),
            pltpu.VMEM((block, wide), BF16),
            pltpu.VMEM((sec, block, wide), BF16),
            pltpu.VMEM((block, wide), BF16),
            pltpu.VMEM((block, wide), BF16),
            pltpu.VMEM((sec, block, wide), BF16),
            pltpu.VMEM((2, block, wide), BF16),
            pltpu.VMEM((sec, block, wide), BF16),
            pltpu.SemaphoreType.DMA((3,)),
            pltpu.SemaphoreType.DMA((sec,)),
            pltpu.SemaphoreType.DMA((len(chunks), len(PIECES))),
            pltpu.SemaphoreType.DMA((len(chunks), len(PIECES))),
            pltpu.SemaphoreType.DMA((sec,)),
            pltpu.SemaphoreType.DMA((sec,)),
            pltpu.SemaphoreType.DMA((n_msg,)),
            pltpu.SemaphoreType.DMA((n_msg,)),
            pltpu.SemaphoreType.DMA((n_msg,)),
            pltpu.SemaphoreType.REGULAR,
        ],
        compiler_params=pltpu.CompilerParams(collective_id=0, has_side_effects=True),
    )(local_ops.transpose(1, 2, 0), targets.T, wavefunction, left_env, right_env)


def solution(mesh):
    return jax.shard_map(
        local,
        mesh=mesh,
        in_specs=(
            P("dom", "sec", None, None, None),
            P("dom", None, "sec", None, None),
            P("dom", None, "sec", None, None),
            P(),
            P(),
        ),
        out_specs=P("dom", "sec", None, None, None),
        check_vma=False,
    )
```
